32 devices in a mesh: groups: 2 (over y), pulse: 4 (over x, core), range: 4 (over z).
Axes of the slice: x: 2, y: 2, z: 4, core: 2. Of those that a mesh axis runs over, the one named last changes fastest.
Arguments:
- echoes: bfloat16 [2048, 2, 8192], P(('groups', 'pulse'), None, 'range'), parts along dimension 0, may hold values from -6 to 6
- shifts: int32 [2048], P(('groups', 'pulse')), parts along dimension 0, may hold values from -64 to 64
- tap_weights: float32 [2048, 8], P(('groups', 'pulse')), parts along dimension 0, may hold values from -2 to 2
- angles: float32 [2048], P(('groups', 'pulse')), parts along dimension 0, may hold values from -3.140625 to 3.140625
- slopes: float32 [2048], P(('groups', 'pulse')), parts along dimension 0, may hold values from -0.05 to 0.05
- steering: bfloat16 [2, 8, 32], replicated, may hold values from -0.75 to 0.75
- footprint: int32 [32, 32], P('groups'), parts along dimension 0, may hold values from 0 to 255, as said below
- tile_coeffs: bfloat16 [32, 2, 64, 32], P(('groups', 'pulse')), parts along dimension 0, may hold values from -0.75 to 0.75
Outputs:
- image_tiles: bfloat16 [32, 2, 64, 8192], P(('groups', 'pulse'), None, None, 'range'), parts along dimension 0
The draws below stay inside these ranges and needn't reach their ends.
There are 2 independent parts, one for each index of `groups`. The reference program is written for one: setup_inputs(seed, part) draws one part's arguments, and reference() takes and returns one part's arrays. A program takes and returns all parts, laid end to end along the dimension named above; an argument that names none is the same for every part. Nothing has to cross between parts.
Inputs may be any that keep to these rules, and one draw needn't show every extreme that they name: `footprint`: beam s * 8 + b belongs to subaperture s. The 128 entries of tiles k * 4 to k * 4 + 3 are distinct beams; at most 64 of them lie in any one range of beams j * 64 to j * 64 + 63, and for every k exactly 64 lie in some such range.
All inputs are finite; a program needn't handle non-finite values.
Results may differ from the reference program's by a relative error of at most 0.0058.
Values may be sent and summed in bfloat16 or wider, within the bound.
No kernel may reach another device: no remote copies, remote signals or barrier semaphores. Data moves between devices by JAX's collectives and lax.ppermute only.
A program may use at most 64 MiB of HBM per device.

```python
import jax
import jax.numpy as jnp
from jax import lax

SUB = 32
BEAMS = 8
TAPS = 8
MAXS = 64
TILE_DEV = 4
FOOT = 32
AZ = 64
PULSES = 1024
RANGE = 8192
NT = 16
BEAM_DEV = 64
NBEAMS = 256
ENT = 128
CAP = 64
HALO = 68
N_PULSE = 4


def draw_footprint(key, part):
    average = ENT // N_PULSE

    def one_owner(owner):
        owner_key = jax.random.fold_in(key, owner)
        k_pairs, k_order, k_pick, k_mix = jax.random.split(owner_key, 4)
        spread = jax.random.randint(k_pairs, (N_PULSE // 2,), 0, average // 2 + 1)
        spread = spread.at[0].set(average)
        counts = jnp.stack([average + spread, average - spread], axis=1).reshape(N_PULSE)
        counts = counts[jax.random.permutation(k_order, N_PULSE)]

        def one_source(source):
            beam_order = jax.random.permutation(jax.random.fold_in(k_pick, source), BEAM_DEV)
            return source * BEAM_DEV + beam_order[:CAP]
        candidates = jax.vmap(one_source)(jnp.arange(N_PULSE, dtype=jnp.int32))
        is_valid = jnp.arange(CAP)[None, :] < counts[:, None]
        flat_ids = candidates.reshape(N_PULSE * CAP)
        flat_valid = is_valid.reshape(N_PULSE * CAP)
        ranking = jnp.argsort(jnp.where(flat_valid, 0, 1), stable=True)[:ENT]
        chosen = flat_ids[ranking]
        return chosen[jax.random.permutation(k_mix, ENT)].reshape(TILE_DEV, FOOT)
    owners = jax.vmap(one_owner)(jnp.arange(N_PULSE, dtype=jnp.int32))
    return owners.reshape(N_PULSE * TILE_DEV, FOOT).astype(jnp.int32)


def touch_ends(drawn, own_key, low, high):
    longest = drawn.shape.index(max(drawn.shape))
    spots = []
    for shift in (0, 1):
        where = [jax.random.randint(jax.random.fold_in(own_key, axis), (), 0, length) for axis, length in enumerate(drawn.shape)]
        where[longest] = (where[longest] + shift) % drawn.shape[longest]
        spots.append(tuple(where))
    return drawn.at[spots[0]].set(low).at[spots[1]].set(high)


def levels(stream_key, dims, cuts, smallest, largest):
    gain = 1.0
    for position, blocks in cuts:
        draws = jax.random.uniform(jax.random.fold_in(jax.random.fold_in(stream_key, 6), position), (blocks,), jnp.float32, smallest / len(cuts), largest / len(cuts))
        gain = gain * jnp.repeat(jnp.exp(draws), dims[position] // blocks).reshape((-1,) + (1,) * (len(dims) - 1 - position))
    return gain


def normal_values(key, shape, width, bound, cuts=(), kind=jnp.bfloat16):
    array = jax.random.normal(key, shape, jnp.float32) * width
    if len(cuts) > 0:
        array = levels(key, shape, cuts, -0.22, 0.18) * array
    return jnp.clip(array, min=-bound, max=bound).astype(kind)


def setup_inputs(seed: int = 0, part: int = 0) -> dict:
    arg_keys = jax.random.split(jax.random.key(seed), 9)
    own_keys = jax.random.split(jax.random.fold_in(arg_keys[8], part), 9)
    echoes = normal_values(own_keys[0], (PULSES, 2, RANGE), 1.0, 6.0, ((0, 4), (2, 4)))
    shifts = touch_ends(jax.random.randint(own_keys[1], (PULSES,), 0 - MAXS, MAXS + 1), jax.random.fold_in(own_keys[1], 1), 0 - MAXS, MAXS).astype(jnp.int32)
    tap_weights = normal_values(own_keys[2], (PULSES, TAPS), 0.35, 2.0, ((0, 4),), jnp.float32)
    angles = jnp.clip(jax.random.uniform(own_keys[3], (PULSES,), jnp.float32, -3.140625, 3.140625), -3.140625, 3.140625)
    slopes = jnp.clip(jax.random.uniform(own_keys[4], (PULSES,), jnp.float32, -0.05, 0.05) * levels(own_keys[4], (PULSES,), ((0, 4),), -0.4, 0.0), -0.05, 0.05)
    steering = normal_values(arg_keys[5], (2, BEAMS, SUB), (2 * SUB) ** -0.5, 0.75)
    footprint = draw_footprint(jax.random.fold_in(jax.random.fold_in(arg_keys[8], part), 71), part)
    tile_coeffs = normal_values(own_keys[7], (NT, 2, AZ, FOOT), (2 * FOOT) ** -0.5, 0.75, ((0, 4),))
    return {"echoes": echoes, "shifts": shifts, "tap_weights": tap_weights, "angles": angles, "slopes": slopes, "steering": steering, "footprint": footprint, "tile_coeffs": tile_coeffs}


def align_pulse(pulse_row, bin_offset, tap_row, phase_zero, phase_slope, start_cell):
    span_cells = pulse_row.shape[1] - 2 * HALO
    first_cell = (HALO + bin_offset - TAPS // 2 + 1).astype(jnp.int32)
    window = lax.dynamic_slice(pulse_row, (jnp.int32(0), first_cell), (2, span_cells + TAPS - 1)).astype(jnp.float32)
    summed = jnp.zeros((2, span_cells), jnp.float32)
    for tap_index in range(TAPS):
        summed = summed + tap_row[tap_index] * window[:, tap_index:tap_index + span_cells]
    positions = (start_cell + jnp.arange(span_cells)).astype(jnp.float32)
    phases = phase_zero + phase_slope * positions
    cosine_values = jnp.cos(phases)
    sine_values = jnp.sin(phases)
    real_part = cosine_values * summed[0] - sine_values * summed[1]
    imag_part = sine_values * summed[0] + cosine_values * summed[1]
    return jnp.stack([real_part, imag_part]).astype(jnp.bfloat16)


def reference(echoes, shifts, tap_weights, angles, slopes, steering, footprint, tile_coeffs):
    padded = jnp.pad(echoes, ((0, 0), (0, 0), (HALO, HALO)))
    aligner = jax.vmap(align_pulse, in_axes=(0, 0, 0, 0, 0, None))

    def one_sub(sub_index):
        first_pulse = (sub_index * SUB).astype(jnp.int32)
        rows = lax.dynamic_slice_in_dim(padded, first_pulse, SUB, 0)
        offsets = lax.dynamic_slice_in_dim(shifts, first_pulse, SUB, 0)
        tap_rows = lax.dynamic_slice_in_dim(tap_weights, first_pulse, SUB, 0)
        zeros_at = lax.dynamic_slice_in_dim(angles, first_pulse, SUB, 0)
        slope_at = lax.dynamic_slice_in_dim(slopes, first_pulse, SUB, 0)
        aligned = aligner(rows, offsets, tap_rows, zeros_at, slope_at, jnp.int32(0))
        real_in = aligned[:, 0]
        imag_in = aligned[:, 1]
        real_part = jnp.dot(steering[0], real_in, preferred_element_type=jnp.float32) - jnp.dot(steering[1], imag_in, preferred_element_type=jnp.float32)
        imag_part = jnp.dot(steering[0], imag_in, preferred_element_type=jnp.float32) + jnp.dot(steering[1], real_in, preferred_element_type=jnp.float32)
        return jnp.stack([real_part, imag_part], axis=1).astype(jnp.bfloat16)

    beam_rows = lax.map(one_sub, jnp.arange(PULSES // SUB, dtype=jnp.int32))
    beam_rows = beam_rows.reshape(NBEAMS, 2, RANGE)

    def one_tile(pair):
        beam_ids, tile_coeff = pair
        picked = jnp.take(beam_rows, beam_ids, axis=0).astype(jnp.float32)
        weights = tile_coeff.astype(jnp.float32)
        real_part = jnp.einsum('af,fw->aw', weights[0], picked[:, 0]) - jnp.einsum('af,fw->aw', weights[1], picked[:, 1])
        imag_part = jnp.einsum('af,fw->aw', weights[0], picked[:, 1]) + jnp.einsum('af,fw->aw', weights[1], picked[:, 0])
        return jnp.stack([real_part, imag_part]).astype(jnp.bfloat16)

    return lax.map(one_tile, (footprint, tile_coeffs))
```

```python
import functools

import jax
import jax.numpy as jnp
from jax import lax
from jax.experimental import pallas as pl
from jax.experimental.pallas import tpu as pltpu
from jax.sharding import PartitionSpec as P

SUB = 32
BEAMS = 8
TAPS = 8
TILE_DEV = 4
FOOT = 32
AZ = 64
LANES = 128
ROWS = 264
GROUP = 128
UNROLL = 16


def beam_kernel(slots, first_row, segments, pulses, shift_ref, x_hbm, table_ref, factor_ref, steer_ref, out_ref, xbuf, aligned, demod, weights, products, sems):
    rows = 2 * slots
    subs = pulses // SUB

    def fetch(sub):
        window = pl.ds(sub * SUB, SUB)
        return pltpu.make_async_copy(
            x_hbm.at[window, pl.ds(first_row, rows), :], xbuf.at[window], sems.at[sub]
        )

    for sub in range(subs):
        fetch(sub).start()
    lane = lax.broadcasted_iota(jnp.int32, (rows, LANES), 1)
    for sub in range(subs):
        fetch(sub).wait()

        def align(step, carry, sub=sub):
            for inner in range(UNROLL):
                pulse = sub * SUB + step * UNROLL + inner
                offset = shift_ref[pulse] - 3
                rest = offset & (LANES - 1)
                block = offset >> 7
                here = xbuf[pulse].astype(jnp.float32)
                after = pltpu.roll(here, rows - 2, 0)
                mixed = jnp.where(lane >= rest, here, after)
                turned = pltpu.roll(mixed, (LANES - rest) & (LANES - 1), 1)
                aligned[pl.ds(pulse - 2 * block * ROWS, rows, stride=ROWS), :] = turned
            return carry

        lax.fori_loop(0, SUB // UNROLL, align, 0)

    lane8 = lax.broadcasted_iota(jnp.int32, (8, LANES), 1)
    steer_re, steer_im = steer_ref[0], steer_ref[1]
    for group in range(pulses // GROUP):
        window = pl.ds(group * GROUP, GROUP)
        base_cos, base_sin = table_ref[0, window, :], table_ref[1, window, :]
        cos_a, sin_a = base_cos[:, 127:128], base_sin[:, 127:128]
        cos_b, sin_b = base_cos[:, 1:2], base_sin[:, 1:2]
        step_cos = jnp.broadcast_to(cos_a * cos_b - sin_a * sin_b, (GROUP, LANES))
        step_sin = jnp.broadcast_to(sin_a * cos_b + cos_a * sin_b, (GROUP, LANES))
        for slot, blocks, region, column in segments:
            for tap in range(TAPS):
                fac_re = factor_ref[region, 0, tap : tap + 1, window]
                fac_im = factor_ref[region, 1, tap : tap + 1, window]
                w_re = steer_re * fac_re - steer_im * fac_im
                w_im = steer_re * fac_im + steer_im * fac_re
                for sub in range(GROUP // SUB):
                    keep = (lane8 >= sub * SUB) & (lane8 < (sub + 1) * SUB)
                    p_re = jnp.where(keep, w_re, 0.0)
                    p_im = jnp.where(keep, w_im, 0.0)
                    top = jnp.concatenate([p_re, 0.0 - p_im], axis=1)
                    low = jnp.concatenate([p_im, p_re], axis=1)
                    weights[pl.ds(tap * 64 + sub * 16, 16), :] = jnp.concatenate(
                        [top, low], axis=0
                    ).astype(jnp.bfloat16)
            cos_now, sin_now = base_cos, base_sin
            for block in range(blocks + 1):
                at = 2 * (slot + block) * ROWS + group * GROUP
                real = aligned[pl.ds(at, GROUP), :]
                imag = aligned[pl.ds(at + ROWS, GROUP), :]
                here = pl.ds(block * LANES, LANES)
                demod[0:GROUP, here] = (real * cos_now - imag * sin_now).astype(jnp.bfloat16)
                demod[GROUP : 2 * GROUP, here] = (real * sin_now + imag * cos_now).astype(jnp.bfloat16)
                if block < blocks:
                    cos_now, sin_now = (
                        cos_now * step_cos - sin_now * step_sin,
                        sin_now * step_cos + cos_now * step_sin,
                    )
            width = (blocks + 1) * LANES
            for start in range(0, width, 256):
                here = pl.ds(start, min(256, width - start))
                products[:, here] = jnp.dot(
                    weights[...], demod[:, here], preferred_element_type=jnp.float32
                )

            def combine(step, carry, blocks=blocks, group=group, column=column):
                row = pl.multiple_of(step * 8, 8)
                later = None
                for block in range(blocks, -1, -1):
                    turned = []
                    for tap in range(TAPS):
                        piece = products[pl.ds(tap * 64 + row, 8), pl.ds(block * LANES, LANES)]
                        turned.append(pltpu.roll(piece, LANES - tap, 1) if tap else piece)
                    if later is not None:
                        total = turned[0]
                        for tap in range(1, TAPS):
                            total = total + jnp.where(lane8 < LANES - tap, turned[tap], later[tap])
                        out_ref[pl.ds(group * 64 + row, 8), pl.ds(column + block * LANES, LANES)] = (
                            total.astype(jnp.bfloat16)
                        )
                    later = turned
                return carry

            lax.fori_loop(0, 8, combine, 0)


def make_beams(x3, shifts, table, factors, steer, slots, first_row, segments, name):
    pulses = x3.shape[0]
    blocks = max(seg[1] for seg in segments)
    width = sum(seg[1] for seg in segments) * LANES
    return pl.pallas_call(
        functools.partial(beam_kernel, slots, first_row, segments, pulses),
        name=name,
        out_shape=jax.ShapeDtypeStruct((pulses // 2, width), jnp.bfloat16),
        in_specs=[
            pl.BlockSpec(memory_space=pltpu.SMEM),
            pl.BlockSpec(memory_space=pl.ANY),
            pl.BlockSpec(memory_space=pltpu.VMEM),
            pl.BlockSpec(memory_space=pltpu.VMEM),
            pl.BlockSpec(memory_space=pltpu.VMEM),
        ],
        out_specs=pl.BlockSpec(memory_space=pltpu.VMEM),
        scratch_shapes=[
            pltpu.VMEM((pulses, 2 * slots, LANES), jnp.bfloat16),
            pltpu.VMEM((2 * (slots + 1) * ROWS, LANES), jnp.float32),
            pltpu.VMEM((2 * GROUP, (blocks + 1) * LANES), jnp.bfloat16),
            pltpu.VMEM((64 * TAPS, 2 * GROUP), jnp.bfloat16),
            pltpu.VMEM((64 * TAPS, (blocks + 1) * LANES), jnp.float32),
            pltpu.SemaphoreType.DMA((pulses // SUB,)),
        ],
        cost_estimate=pl.CostEstimate(flops=2000000000, bytes_accessed=8000000, transcendentals=0),
    )(shifts, x3, table, factors, steer)


def expand_kernel(where_ref, coeff_ref, out_ref):
    width = out_ref.shape[1]
    lane = lax.broadcasted_iota(jnp.int32, (FOOT, width), 1)
    dims = (((0,), (0,)), ((), ()))
    for tile in range(TILE_DEV):
        spot = where_ref[pl.ds(tile * FOOT, FOOT), :]
        hot_re = (lane == spot).astype(jnp.float32).astype(jnp.bfloat16)
        hot_im = (lane == spot + BEAMS).astype(jnp.float32).astype(jnp.bfloat16)
        c_re, c_im = coeff_ref[tile, 0], coeff_ref[tile, 1]
        dot = functools.partial(lax.dot_general, dimension_numbers=dims, preferred_element_type=jnp.float32)
        at = tile * 2 * AZ
        out_ref[pl.ds(at, AZ), :] = (dot(c_re, hot_re) - dot(c_im, hot_im)).astype(jnp.bfloat16)
        out_ref[pl.ds(at + AZ, AZ), :] = (dot(c_im, hot_re) + dot(c_re, hot_im)).astype(jnp.bfloat16)


def project_kernel(count, pieces, coeff_ref, *refs):
    sources = refs[:count]
    out_hbm, tile, sems = refs[-3], refs[-2], refs[-1]
    depth = sources[0].shape[0]
    copies = []
    for index, (source, target, width) in enumerate(pieces):
        for start in range(0, width, 256):
            size = min(256, width - start)
            here = pl.ds(source + start, size)
            total = None
            for first in range(0, count, 2):
                data = jnp.concatenate([ref[:, here] for ref in sources[first : first + 2]], axis=0)
                term = jnp.dot(
                    coeff_ref[:, first * depth : (first + 2) * depth], data, preferred_element_type=jnp.float32
                )
                total = term if total is None else total + term
            tile[:, here] = total.astype(jnp.bfloat16)
        copy = pltpu.make_async_copy(
            tile.at[:, pl.ds(source, width)], out_hbm.at[:, pl.ds(target, width)], sems.at[index]
        )
        copy.start()
        copies.append(copy)
    for copy in copies:
        copy.wait()


def project(coeffs, sources, image, pieces, cells, name):
    count = len(sources)
    width = sources[0].shape[1]
    rows = coeffs.shape[0]
    any_spec = pl.BlockSpec(memory_space=pl.ANY)
    vmem = pl.BlockSpec(memory_space=pltpu.VMEM)
    extra = [] if image is None else [image]
    return pl.pallas_call(
        functools.partial(project_kernel, count, pieces),
        name=name,
        out_shape=jax.ShapeDtypeStruct((rows, cells), jnp.bfloat16),
        in_specs=[vmem] * (1 + count) + [any_spec] * len(extra),
        out_specs=any_spec,
        input_output_aliases={1 + count: 0} if extra else {},
        scratch_shapes=[
            pltpu.VMEM((rows, width), jnp.bfloat16),
            pltpu.SemaphoreType.DMA((len(pieces),)),
        ],
        cost_estimate=pl.CostEstimate(
            flops=2 * rows * width * count * sources[0].shape[0], bytes_accessed=3000000, transcendentals=0
        ),
    )(coeffs, *sources, *extra)


def body(echoes, shifts, tap_weights, angles, slopes, steering, footprint, tile_coeffs):
    pulses, _, cells = echoes.shape
    blocks = cells // LANES
    pulse_count = lax.axis_size("pulse")
    range_count = lax.axis_size("range")
    me = lax.axis_index("pulse")
    start_cell = lax.axis_index("range") * cells

    x4 = echoes.reshape(pulses, 2, blocks, LANES).transpose(0, 2, 1, 3)
    ends = range_count - 1
    left = lax.ppermute(x4[:, blocks - 1 :], "range", [(i, i + 1) for i in range(ends)])
    right = lax.ppermute(x4[:, :1], "range", [(i + 1, i) for i in range(ends)])

    half = blocks // 2
    origins = [1, half - 1, 0, blocks - 1]
    taps = jnp.arange(TAPS, dtype=jnp.int32)
    cell = (start_cell + LANES * jnp.array(origins, dtype=jnp.int32)[:, None] - taps[None, :]).astype(jnp.float32)
    phases = angles[None, None, :] + slopes[None, None, :] * cell[:, :, None]
    tap_rows = tap_weights.T[None]
    factors = jnp.stack([tap_rows * jnp.cos(phases), tap_rows * jnp.sin(phases)], axis=1)
    turn = slopes[:, None] * jnp.arange(LANES, dtype=jnp.float32)[None, :]
    table = jnp.stack([jnp.cos(turn), jnp.sin(turn)])
    steer = jnp.tile(steering.astype(jnp.float32), (1, 1, GROUP // SUB))

    x3 = x4.reshape(pulses, 2 * blocks, LANES)
    beams = [
        make_beams(x3, shifts, table, factors, steer, half, 0, ((1, half - 2, 0, 0),), "beams_a"),
        make_beams(x3, shifts, table, factors, steer, half + 4, 2 * (half - 4), ((3, half, 1, 0),), "beams_b"),
    ]
    edge = jnp.concatenate([left, x4[:, :3], x4[:, blocks - 3 :], right], axis=1)
    edge = edge.reshape(pulses, 16, LANES)
    beams.append(
        make_beams(edge, shifts, table, factors, steer, 8, 0, ((1, 1, 2, 0), (6, 1, 3, LANES)), "beams_c")
    )
    inner = (half - 2) * LANES
    pieces = [
        ((0, LANES, inner),),
        ((0, (half - 1) * LANES, half * LANES),),
        ((0, 0, LANES), (LANES, (blocks - 1) * LANES, LANES)),
    ]

    entries = TILE_DEV * FOOT
    chips = pulse_count // 2
    beam_dev = pulses // SUB * BEAMS
    ids = lax.dynamic_index_in_dim(footprint.reshape(pulse_count, entries), me, 0, keepdims=False)
    owner = ids // beam_dev
    inside = ids % beam_dev
    place = 2 * ((me // 2 - owner // 2) % chips) + (me % 2 + owner % 2) % 2
    where = place * (2 * beam_dev) + (inside // BEAMS) * (2 * BEAMS) + inside % BEAMS
    coeffs = pl.pallas_call(
        expand_kernel,
        name="expand",
        out_shape=jax.ShapeDtypeStruct((TILE_DEV * 2 * AZ, pulse_count * 2 * beam_dev), jnp.bfloat16),
    )(where[:, None], tile_coeffs.transpose(0, 1, 3, 2))

    swap = [(i, i ^ 1) for i in range(pulse_count)]
    image = None
    for index, own in enumerate(beams):
        sources = []
        for hop in range(chips):
            ahead = own
            if hop:
                ahead = lax.ppermute(own, "pulse", [(i, (i + 2 * hop) % pulse_count) for i in range(pulse_count)])
            sources += [ahead, lax.ppermute(ahead, "pulse", swap)]
        image = project(coeffs, sources, image, pieces[index], cells, "project_" + "abc"[index])
    return image.reshape(TILE_DEV, 2, AZ, cells)


def solution(mesh):
    placed = (
        P(("groups", "pulse"), None, "range"),
        P(("groups", "pulse")),
        P(("groups", "pulse"), None),
        P(("groups", "pulse")),
        P(("groups", "pulse")),
        P(),
        P("groups", None),
        P(("groups", "pulse"), None, None, None),
    )
    return jax.shard_map(
        body,
        mesh=mesh,
        in_specs=placed,
        out_specs=P(("groups", "pulse"), None, None, "range"),
        check_vma=False,
    )
```

```python
import functools

import jax
import jax.numpy as jnp
from jax import lax
from jax.experimental import pallas as pl
from jax.experimental.pallas import tpu as pltpu
from jax.sharding import PartitionSpec as P

SUB = 32
BEAMS = 8
TAPS = 8
TILE_DEV = 4
FOOT = 32
AZ = 64
LANES = 128
ROWS = 264
GROUP = 128
NEAR = 5


def fetch_sub(x_hbm, xbuf, sems, sub):
    window = pl.ds(pl.multiple_of(sub * SUB, SUB), SUB)
    return pltpu.make_async_copy(x_hbm.at[window], xbuf.at[window], sems.at[sub])


def align_all(rows, subs, shift_ref, x_hbm, xbuf, aligned, sems):
    lane = lax.broadcasted_iota(jnp.int32, (rows, LANES), 1)

    def align(sub, carry):
        fetch_sub(x_hbm, xbuf, sems, sub).wait()
        for inner in range(SUB):
            pulse = sub * SUB + inner
            raised = shift_ref[pulse] + (LANES - 3)
            rest = raised & (LANES - 1)
            here = xbuf[pulse].astype(jnp.float32)
            after = pltpu.roll(here, rows - 2, 0)
            mixed = jnp.where(lane >= rest, here, after)
            turned = pltpu.roll(mixed, (LANES - rest) & (LANES - 1), 1)
            first = pulse + 2 * ROWS * (1 - (raised >> 7))
            aligned[pl.ds(first, rows, stride=ROWS), :] = turned
        return carry

    lax.fori_loop(0, subs, align, 0)


def turn_by(a, b):
    return a[0] * b[0] - a[1] * b[1], a[0] * b[1] + a[1] * b[0]


def read_demod(aligned, slot, group, phase):
    at = 2 * slot * ROWS + group * GROUP
    real = aligned[pl.ds(at, GROUP), :]
    imag = aligned[pl.ds(at + ROWS, GROUP), :]
    real, imag = turn_by((real, imag), phase)
    return jnp.concatenate([real, imag], axis=0).astype(jnp.bfloat16)


def multiply(weights, demod, products, width):
    for start in range(0, width, 256):
        here = pl.ds(start, min(256, width - start))
        products[:, here] = jnp.dot(weights[...], demod[:, here], preferred_element_type=jnp.float32)


def combine(products, out_ref, group, runs):
    lane = lax.broadcasted_iota(jnp.int32, (8, LANES), 1)
    for row in range(0, 64, 8):
        for first, blocks, column in runs:
            later = None
            for block in range(blocks, -1, -1):
                turned = []
                for tap in range(TAPS):
                    piece = products[pl.ds(tap * 64 + row, 8), pl.ds((first + block) * LANES, LANES)]
                    turned.append(pltpu.roll(piece, LANES - tap, 1) if tap else piece)
                if later is not None:
                    total = turned[0]
                    for tap in range(1, TAPS):
                        total = total + jnp.where(lane < LANES - tap, turned[tap], later[tap])
                    here = pl.ds(column + block * LANES, LANES)
                    out_ref[pl.ds(group * 64 + row, 8), here] = total.astype(jnp.bfloat16)
                later = turned


def front_kernel(near, far, start_ref, shift_ref, x_hbm, tap_ref, angle_ref, slope_ref, steer_ref, out_ref, far_ref, weight_ref, phase_ref, xbuf, aligned, demod, products, sems):
    pulses = shift_ref.shape[0]
    subs = pulses // SUB
    for sub in range(subs):
        fetch_sub(x_hbm, xbuf, sems, sub).start()

    slope = slope_ref[...]
    row = lax.broadcasted_iota(jnp.int32, (8, pulses), 0)
    cell = (start_ref[0] - row).astype(jnp.float32)
    factor_arg = angle_ref[...] + slope * cell
    factor_re = tap_ref[...] * jnp.cos(factor_arg)
    factor_im = tap_ref[...] * jnp.sin(factor_arg)
    low = slope * row.astype(jnp.float32)
    rows = [(jnp.cos(low), jnp.sin(low))]
    power = slope * jnp.left_shift(8, row).astype(jnp.float32)
    power_cos, power_sin = jnp.cos(power), jnp.sin(power)
    for bit in range(4):
        by = power_cos[bit : bit + 1], power_sin[bit : bit + 1]
        rows = rows + [turn_by(item, by) for item in rows]
    base_cos = jnp.concatenate([item[0] for item in rows], axis=0).T
    base_sin = jnp.concatenate([item[1] for item in rows], axis=0).T

    lane8 = lax.broadcasted_iota(jnp.int32, (8, LANES), 1)
    steer_re = jnp.concatenate([steer_ref[0].astype(jnp.float32)] * (GROUP // SUB), axis=1)
    steer_im = jnp.concatenate([steer_ref[1].astype(jnp.float32)] * (GROUP // SUB), axis=1)
    groups = pulses // GROUP
    for group in range(groups):
        here = slice(group * GROUP, (group + 1) * GROUP)
        for tap in range(TAPS):
            factor = factor_re[tap : tap + 1, here], factor_im[tap : tap + 1, here]
            w_re, w_im = turn_by((steer_re, steer_im), factor)
            for sub in range(GROUP // SUB):
                keep = (lane8 >= sub * SUB) & (lane8 < (sub + 1) * SUB)
                p_re = jnp.where(keep, w_re, 0.0)
                p_im = jnp.where(keep, w_im, 0.0)
                top = jnp.concatenate([p_re, 0.0 - p_im], axis=1)
                bottom = jnp.concatenate([p_im, p_re], axis=1)
                weight_ref[group, pl.ds(tap * 64 + sub * 16, 16), :] = jnp.concatenate(
                    [top, bottom], axis=0
                ).astype(jnp.bfloat16)

    align_all(xbuf.shape[1], subs, shift_ref, x_hbm, xbuf, aligned, sems)

    for group in range(groups):
        here = slice(group * GROUP, (group + 1) * GROUP)
        phase = base_cos[here], base_sin[here]
        step = turn_by((phase[0][:, 127:128], phase[1][:, 127:128]), (phase[0][:, 1:2], phase[1][:, 1:2]))
        step = jnp.broadcast_to(step[0], (GROUP, LANES)), jnp.broadcast_to(step[1], (GROUP, LANES))
        last = near + far + 1
        for block in range(last + 2):
            if block in (0, 1, last, last + 1):
                spot = (0, 1, last, last + 1).index(block)
                phase_ref[spot, 0, here, :] = phase[0]
                phase_ref[spot, 1, here, :] = phase[1]
            if 1 <= block <= last:
                data = read_demod(aligned, block, group, phase)
                if block <= near + 1:
                    demod[group, :, pl.ds((block - 1) * LANES, LANES)] = data
                if block >= near + 1:
                    far_ref[group, :, pl.ds((block - near - 1) * LANES, LANES)] = data
            phase = turn_by(phase, step)
        multiply(weight_ref.at[group], demod.at[group], products.at[group], (near + 1) * LANES)
    for group in range(groups):
        combine(products.at[group], out_ref, group, ((0, near, 0),))


def middle_kernel(far, demod_ref, weight_ref, out_ref, products):
    groups = weight_ref.shape[0]
    for group in range(groups):
        multiply(weight_ref.at[group], demod_ref.at[group], products.at[group], (far + 1) * LANES)
    for group in range(groups):
        combine(products.at[group], out_ref, group, ((0, far, 0),))


def edge_kernel(shift_ref, x_hbm, weight_ref, phase_ref, out_ref, xbuf, aligned, demod, products, sems):
    pulses = shift_ref.shape[0]
    subs = pulses // SUB
    for sub in range(subs):
        fetch_sub(x_hbm, xbuf, sems, sub).start()
    align_all(xbuf.shape[1], subs, shift_ref, x_hbm, xbuf, aligned, sems)
    groups = pulses // GROUP
    for group in range(groups):
        here = pl.ds(group * GROUP, GROUP)
        for spot, slot in enumerate((1, 2, 6, 7)):
            phase = phase_ref[spot, 0, here, :], phase_ref[spot, 1, here, :]
            demod[group, :, pl.ds(spot * LANES, LANES)] = read_demod(aligned, slot, group, phase)
        multiply(weight_ref.at[group], demod.at[group], products.at[group], 4 * LANES)
    for group in range(groups):
        combine(products.at[group], out_ref, group, ((0, 1, 0), (2, 1, LANES)))


def beam_scratch(pulses, rows, blocks):
    groups = pulses // GROUP
    return [
        pltpu.VMEM((pulses, rows, LANES), jnp.bfloat16),
        pltpu.VMEM(((rows + 2) * ROWS, LANES), jnp.float32),
        pltpu.VMEM((groups, 2 * GROUP, blocks * LANES), jnp.bfloat16),
        pltpu.VMEM((groups, 64 * TAPS, blocks * LANES), jnp.float32),
        pltpu.SemaphoreType.DMA((pulses // SUB,)),
    ]


SMEM = pl.BlockSpec(memory_space=pltpu.SMEM)
VMEM = pl.BlockSpec(memory_space=pltpu.VMEM)
ANY = pl.BlockSpec(memory_space=pl.ANY)


def make_beams(x3, start, shifts, tap_rows, angles, slopes, steering, near):
    pulses, rows, _ = x3.shape
    far = rows // 2 - 2 - near
    groups = pulses // GROUP
    out = jax.ShapeDtypeStruct
    first, rest, weights, phases = pl.pallas_call(
        functools.partial(front_kernel, near, far),
        name="front",
        out_shape=(
            out((pulses // 2, near * LANES), jnp.bfloat16),
            out((groups, 2 * GROUP, (far + 1) * LANES), jnp.bfloat16),
            out((groups, 64 * TAPS, 2 * GROUP), jnp.bfloat16),
            out((4, 2, pulses, LANES), jnp.float32),
        ),
        in_specs=[SMEM, SMEM, ANY, VMEM, VMEM, VMEM, VMEM],
        out_specs=(VMEM, VMEM, VMEM, VMEM),
        scratch_shapes=beam_scratch(pulses, rows, near + 1),
        cost_estimate=pl.CostEstimate(flops=3000000000, bytes_accessed=8000000, transcendentals=0),
    )(start, shifts, x3, tap_rows, angles, slopes, steering)
    second = pl.pallas_call(
        functools.partial(middle_kernel, far),
        name="middle",
        out_shape=out((pulses // 2, far * LANES), jnp.bfloat16),
        in_specs=[VMEM, VMEM],
        out_specs=VMEM,
        scratch_shapes=[pltpu.VMEM((groups, 64 * TAPS, (far + 1) * LANES), jnp.float32)],
        cost_estimate=pl.CostEstimate(flops=2000000000, bytes_accessed=4000000, transcendentals=0),
    )(rest, weights)
    return first, second, weights, phases


def make_edges(edge, shifts, weights, phases):
    pulses, rows, _ = edge.shape
    return pl.pallas_call(
        edge_kernel,
        name="edges",
        out_shape=jax.ShapeDtypeStruct((pulses // 2, 2 * LANES), jnp.bfloat16),
        in_specs=[SMEM, ANY, VMEM, VMEM],
        out_specs=VMEM,
        scratch_shapes=beam_scratch(pulses, rows, 4),
        cost_estimate=pl.CostEstimate(flops=2000000000, bytes_accessed=4000000, transcendentals=0),
    )(shifts, edge, weights, phases)


def expand_kernel(where_ref, coeff_ref, out_ref):
    width = out_ref.shape[1]
    lane = lax.broadcasted_iota(jnp.int32, (FOOT, width), 1)
    dims = (((0,), (0,)), ((), ()))
    for tile in range(TILE_DEV):
        spot = where_ref[pl.ds(tile * FOOT, FOOT), :]
        hot_re = (lane == spot).astype(jnp.float32).astype(jnp.bfloat16)
        hot_im = (lane == spot + BEAMS).astype(jnp.float32).astype(jnp.bfloat16)
        c_re, c_im = coeff_ref[tile, 0], coeff_ref[tile, 1]
        dot = functools.partial(lax.dot_general, dimension_numbers=dims, preferred_element_type=jnp.float32)
        at = tile * 2 * AZ
        out_ref[pl.ds(at, AZ), :] = (dot(c_re, hot_re) - dot(c_im, hot_im)).astype(jnp.bfloat16)
        out_ref[pl.ds(at + AZ, AZ), :] = (dot(c_im, hot_re) + dot(c_re, hot_im)).astype(jnp.bfloat16)


def project_kernel(count, pieces, coeff_ref, *refs):
    sources = refs[:count]
    out_hbm, held, tile, in_sems, sems = refs[-5:]
    depth = sources[0].shape[0]
    loads = [
        pltpu.make_async_copy(ref, held.at[pl.ds(index * depth, depth)], in_sems.at[index])
        for index, ref in enumerate(sources)
    ]
    for load in loads:
        load.start()
    for load in loads:
        load.wait()
    copies = []
    for source, target, width in pieces:
        for start in range(0, width, 256):
            size = min(256, width - start)
            here = pl.ds(source + start, size)
            total = None
            for first in range(0, count, 2):
                window = pl.ds(first * depth, 2 * depth)
                term = jnp.dot(coeff_ref[:, window], held[window, here], preferred_element_type=jnp.float32)
                total = term if total is None else total + term
            tile[:, here] = total.astype(jnp.bfloat16)
            copy = pltpu.make_async_copy(
                tile.at[:, here], out_hbm.at[:, pl.ds(target + start, size)], sems.at[len(copies)]
            )
            copy.start()
            copies.append(copy)
    for copy in copies:
        copy.wait()


def project(coeffs, sources, image, pieces, cells, name):
    count = len(sources)
    depth, width = sources[0].shape
    rows = coeffs.shape[0]
    extra = [] if image is None else [image]
    return pl.pallas_call(
        functools.partial(project_kernel, count, pieces),
        name=name,
        out_shape=jax.ShapeDtypeStruct((rows, cells), jnp.bfloat16),
        in_specs=[VMEM] + [ANY] * (count + len(extra)),
        out_specs=ANY,
        input_output_aliases={1 + count: 0} if extra else {},
        scratch_shapes=[
            pltpu.VMEM((count * depth, width), jnp.bfloat16),
            pltpu.VMEM((rows, width), jnp.bfloat16),
            pltpu.SemaphoreType.DMA((count,)),
            pltpu.SemaphoreType.DMA((sum(-(-piece[2] // 256) for piece in pieces),)),
        ],
        cost_estimate=pl.CostEstimate(
            flops=2 * rows * width * count * depth, bytes_accessed=3000000, transcendentals=0
        ),
    )(coeffs, *sources, *extra)


def body(echoes, shifts, tap_weights, angles, slopes, steering, footprint, tile_coeffs):
    pulses, _, cells = echoes.shape
    blocks = cells // LANES
    pulse_count = lax.axis_size("pulse")
    range_count = lax.axis_size("range")
    me = lax.axis_index("pulse")
    start_cell = lax.axis_index("range") * cells

    x4 = echoes.reshape(pulses, 2, blocks, LANES).transpose(0, 2, 1, 3)
    ends = range_count - 1
    left = lax.ppermute(x4[:, blocks - 1 :], "range", [(i, i + 1) for i in range(ends)])
    right = lax.ppermute(x4[:, :1], "range", [(i + 1, i) for i in range(ends)])

    x3 = x4.reshape(pulses, 2 * blocks, LANES)
    near = NEAR
    first, second, weights, phases = make_beams(
        x3,
        jnp.reshape(start_cell, (1,)),
        shifts,
        tap_weights.T,
        angles[None, :],
        slopes[None, :],
        steering,
        near,
    )
    edge = jnp.concatenate([left, x4[:, :3], x4[:, blocks - 3 :], right], axis=1)
    beams = [first, second, make_edges(edge.reshape(pulses, 16, LANES), shifts, weights, phases)]
    pieces = [
        ((0, LANES, near * LANES),),
        ((0, (near + 1) * LANES, (blocks - 2 - near) * LANES),),
        ((0, 0, LANES), (LANES, (blocks - 1) * LANES, LANES)),
    ]

    entries = TILE_DEV * FOOT
    chips = pulse_count // 2
    beam_dev = pulses // SUB * BEAMS
    ids = lax.dynamic_index_in_dim(footprint.reshape(pulse_count, entries), me, 0, keepdims=False)
    owner = ids // beam_dev
    inside = ids % beam_dev
    place = 2 * ((me // 2 - owner // 2) % chips) + (me % 2 + owner % 2) % 2
    where = place * (2 * beam_dev) + (inside // BEAMS) * (2 * BEAMS) + inside % BEAMS
    coeffs = pl.pallas_call(
        expand_kernel,
        name="expand",
        out_shape=jax.ShapeDtypeStruct((TILE_DEV * 2 * AZ, pulse_count * 2 * beam_dev), jnp.bfloat16),
    )(where[:, None], tile_coeffs.transpose(0, 1, 3, 2))

    swap = [(i, i ^ 1) for i in range(pulse_count)]
    image = None
    for index, own in enumerate(beams):
        sources = []
        for hop in range(chips):
            ahead = own
            if hop:
                ahead = lax.ppermute(own, "pulse", [(i, (i + 2 * hop) % pulse_count) for i in range(pulse_count)])
            sources += [ahead, lax.ppermute(ahead, "pulse", swap)]
        image = project(coeffs, sources, image, pieces[index], cells, "project_" + "abc"[index])
    return image.reshape(TILE_DEV, 2, AZ, cells)


def solution(mesh):
    placed = (
        P(("groups", "pulse"), None, "range"),
        P(("groups", "pulse")),
        P(("groups", "pulse"), None),
        P(("groups", "pulse")),
        P(("groups", "pulse")),
        P(),
        P("groups", None),
        P(("groups", "pulse"), None, None, None),
    )
    return jax.shard_map(
        body,
        mesh=mesh,
        in_specs=placed,
        out_specs=P(("groups", "pulse"), None, None, "range"),
        check_vma=False,
    )
```

```python
import functools

import jax
import jax.numpy as jnp
from jax import lax
from jax.experimental import pallas as pl
from jax.experimental.pallas import tpu as pltpu
from jax.sharding import PartitionSpec as P

SUB = 32
BEAMS = 8
TAPS = 8
TILE_DEV = 4
FOOT = 32
AZ = 64
LANES = 128
STRIDE = 136
GROUP = 128


def turn_by(a, b):
    return a[0] * b[0] - a[1] * b[1], a[0] * b[1] + a[1] * b[0]


def row_of(pair, index):
    return pair[0][index : index + 1], pair[1][index : index + 1]


def angle_pair(value):
    return jnp.cos(value), jnp.sin(value)


def lane_phases(slope):
    row = lax.broadcasted_iota(jnp.int32, (8, GROUP), 0)
    rows = [angle_pair(slope * row.astype(jnp.float32))]
    powers = angle_pair(slope * jnp.left_shift(8, row).astype(jnp.float32))
    for bit in range(4):
        rows = rows + [turn_by(item, row_of(powers, bit)) for item in rows]
    base = tuple(jnp.concatenate([item[part] for item in rows], axis=0).T for part in range(2))
    step = turn_by((base[0][:, 127:128], base[1][:, 127:128]), (base[0][:, 1:2], base[1][:, 1:2]))
    step = tuple(jnp.broadcast_to(part, (GROUP, LANES)) for part in step)
    return base, step


def tap_factors(start_ref, tap_ref, angle, slope, here):
    row = lax.broadcasted_iota(jnp.int32, (8, GROUP), 0)
    cell = (start_ref[0] - LANES - row).astype(jnp.float32)
    cosine, sine = angle_pair(angle + slope * cell)
    taps = tap_ref[:, here]
    return taps * cosine, taps * sine


def fill_weights(factors, steer_ref, weight_ref):
    lane = lax.broadcasted_iota(jnp.int32, (8, LANES), 1)
    steer = tuple(
        jnp.concatenate([steer_ref[part].astype(jnp.float32)] * (GROUP // SUB), axis=1) for part in range(2)
    )
    for tap in range(TAPS):
        w_re, w_im = turn_by(steer, row_of(factors, tap))
        for sub in range(GROUP // SUB):
            keep = (lane >= sub * SUB) & (lane < (sub + 1) * SUB)
            p_re = jnp.where(keep, w_re, 0.0)
            p_im = jnp.where(keep, w_im, 0.0)
            top = jnp.concatenate([p_re, 0.0 - p_im], axis=1)
            bottom = jnp.concatenate([p_im, p_re], axis=1)
            weight_ref[pl.ds(tap * 64 + sub * 16, 16), :] = jnp.concatenate([top, bottom], axis=0).astype(
                jnp.bfloat16
            )


def place_of(shift_ref, pulse, local):
    raised = shift_ref[pulse] + (LANES - 3)
    rest = raised & (LANES - 1)
    return rest, (LANES - rest) & (LANES - 1), local + 2 * STRIDE * (1 - (raised >> 7))


def split_ends(aligned, offset, last):
    lane = lax.broadcasted_iota(jnp.int32, (GROUP, LANES), 1)

    def rows(slot, part):
        return aligned[pl.ds((2 * slot + part) * STRIDE, GROUP), :]

    def first(part):
        return jnp.where(offset >= 0, rows(0, part), jnp.where(lane >= 0 - offset, rows(last + 1, part), 0.0))

    return {
        -1: lambda part: jnp.where(lane >= LANES - offset, rows(last, part), 0.0),
        0: first,
        last: lambda part: jnp.where(lane < LANES - offset, rows(last, part), 0.0),
        last + 1: lambda part: jnp.where(lane < 0 - offset, rows(last + 1, part), 0.0),
    }


def sweep(last, aligned, offset, phase, step, weight_ref, demod, products, carry, store):
    lane = lax.broadcasted_iota(jnp.int32, (8, LANES), 1)
    ends = split_ends(aligned, offset, last)
    for start in range(-1, last + 2, 2):
        for block in (start, start + 1):
            if block in ends:
                data = ends[block](0), ends[block](1)
            else:
                at = 2 * block * STRIDE
                data = aligned[pl.ds(at, GROUP), :], aligned[pl.ds(at + STRIDE, GROUP), :]
            data = turn_by(data, phase)
            phase = turn_by(phase, step)
            here = pl.ds((block + 1) * LANES, LANES)
            demod[:, here] = jnp.concatenate(data, axis=0).astype(jnp.bfloat16)
        here = pl.ds((start + 1) * LANES, 2 * LANES)
        products[:, here] = jnp.dot(weight_ref[...], demod[:, here], preferred_element_type=jnp.float32)
        for row in range(0, 64, 8):
            before = None
            if start >= 0:
                before = [carry[pl.ds(tap * 64 + row, 8), :] for tap in range(TAPS)]
            for block in (start, start + 1):
                turned = []
                for tap in range(TAPS):
                    piece = products[pl.ds(tap * 64 + row, 8), pl.ds((block + 1) * LANES, LANES)]
                    turned.append(pltpu.roll(piece, LANES - tap, 1) if tap else piece)
                if before is not None:
                    total = before[0]
                    for tap in range(1, TAPS):
                        total = total + jnp.where(lane < LANES - tap, before[tap], turned[tap])
                    store(row, block - 1, total)
                before = turned
            if start + 2 < last + 2:
                for tap in range(TAPS):
                    carry[pl.ds(tap * 64 + row, 8), :] = before[tap]
            else:
                total = before[0]
                for tap in range(1, TAPS):
                    total = total + jnp.where(lane < LANES - tap, before[tap], 0.0)
                store(row, last + 1, total)


def fetch_small(sources, targets, sems):
    copies = [pltpu.make_async_copy(s, t, sems.at[i]) for i, (s, t) in enumerate(zip(sources, targets))]
    for copy in copies:
        copy.start()
    return copies


def inner_kernel(group, start_ref, x_hbm, shift_hbm, row_hbm, tap_hbm, angle_hbm, slope_hbm, steer_hbm, *refs):
    if group:
        given_ref, out_ref, below_ref, above_ref, own_ref = refs[:5]
        refs = refs[5:]
    else:
        out_ref, partial_ref = refs[:2]
        refs = refs[2:]
    shift_ref, row_ref, tap_ref, angle_ref, slope_ref, steer_ref, small_sems = refs[:7]
    xbuf, aligned, weights, demod, products, carry, sems = refs[7:]
    small = fetch_small(
        (shift_hbm, row_hbm, tap_hbm, angle_hbm, slope_hbm, steer_hbm),
        (shift_ref, row_ref, tap_ref, angle_ref, slope_ref, steer_ref),
        small_sems,
    )
    first_pulse = group * GROUP
    rows = x_hbm.shape[1]
    fetches = []
    for sub in range(GROUP // SUB):
        window = pl.ds(sub * SUB, SUB)
        fetches.append(
            pltpu.make_async_copy(
                x_hbm.at[pl.ds(first_pulse + sub * SUB, SUB)], xbuf.at[window], sems.at[sub]
            )
        )
        fetches[-1].start()
    for copy in small:
        copy.wait()
    here = slice(first_pulse, first_pulse + GROUP)
    slope, angle = slope_ref[:, here], angle_ref[:, here]
    phase, step = lane_phases(slope)
    fill_weights(tap_factors(start_ref, tap_ref, angle, slope, here), steer_ref, weights)
    offset = jnp.broadcast_to((row_ref[:, here] - 3).astype(jnp.float32), (GROUP, GROUP)).T.astype(jnp.int32)
    lane = lax.broadcasted_iota(jnp.int32, (rows, LANES), 1)
    for local in range(GROUP):
        if local % SUB == 0:
            fetches[local // SUB].wait()
        rest, back, first = place_of(shift_ref, first_pulse + local, local)
        data = xbuf[local].astype(jnp.float32)
        mixed = jnp.where(lane >= rest, data, pltpu.roll(data, rows - 2, 0))
        aligned[pl.ds(first, rows, stride=STRIDE), :] = pltpu.roll(mixed, back, 1)

    last = rows // 2 - 1
    edges = (-1, 0, last, last + 1)

    def store(row, block, total):
        if 0 < block < last:
            out_ref[pl.ds(row, 8), pl.ds((block - 1) * LANES, LANES)] = total.astype(jnp.bfloat16)
            return
        spot = edges.index(block)
        if not group:
            partial_ref[pl.ds(row, 8), pl.ds(spot * LANES, LANES)] = total
            return
        target, column = ((below_ref, 0), (own_ref, 0), (own_ref, LANES), (above_ref, 0))[spot]
        here = pl.ds(column, LANES)
        target[pl.ds(64 + row, 8), here] = total.astype(target.dtype)
        target[pl.ds(row, 8), here] = given_ref[pl.ds(row, 8), pl.ds(spot * LANES, LANES)].astype(target.dtype)

    sweep(last, aligned, offset, phase, step, weights, demod, products, carry, store)


def seal_kernel(ends, place_ref, own_ref, left_ref, right_ref, out_ref):
    for column, ref, outer in ((0, left_ref, 0), (LANES, right_ref, ends)):
        here = pl.ds(column, LANES)
        side = jnp.where(place_ref[0] == outer, 0.0, ref[...].astype(jnp.float32))
        out_ref[:, here] = (own_ref[:, here] + side).astype(jnp.bfloat16)


def grant(mebibytes):
    return pltpu.CompilerParams(vmem_limit_bytes=mebibytes * 1024 * 1024)


SMEM = pl.BlockSpec(memory_space=pltpu.SMEM)
VMEM = pl.BlockSpec(memory_space=pltpu.VMEM)
ANY = pl.BlockSpec(memory_space=pl.ANY)
HBM = pl.BlockSpec(memory_space=pltpu.HBM)


def small_scratch(small):
    spaces = [pltpu.SMEM] + [pltpu.VMEM] * (len(small) - 1)
    return [space(item.shape, item.dtype) for space, item in zip(spaces, small)] + [
        pltpu.SemaphoreType.DMA((len(small),))
    ]


def make_inner(group, start, x3, small, partial=None):
    _, rows, _ = x3.shape
    width = (rows // 2 + 2) * LANES
    inner = jax.ShapeDtypeStruct((64, width - 4 * LANES), jnp.bfloat16)
    if group:
        side = jax.ShapeDtypeStruct((128, LANES), jnp.bfloat16)
        outs = (inner, side, side, jax.ShapeDtypeStruct((128, 2 * LANES), jnp.float32))
        given = (partial,)
    else:
        outs = (inner, jax.ShapeDtypeStruct((64, 4 * LANES), jnp.float32))
        given = ()
    return pl.pallas_call(
        functools.partial(inner_kernel, group),
        out_shape=outs,
        in_specs=[SMEM] + [HBM] * (1 + len(small)) + [VMEM] * len(given),
        out_specs=(VMEM,) * len(outs),
        scratch_shapes=small_scratch(small)
        + [
            pltpu.VMEM((GROUP, rows, LANES), jnp.bfloat16),
            pltpu.VMEM(((rows + 2) * STRIDE, LANES), jnp.float32),
            pltpu.VMEM((64 * TAPS, 2 * GROUP), jnp.bfloat16),
            pltpu.VMEM((2 * GROUP, width), jnp.bfloat16),
            pltpu.VMEM((64 * TAPS, width), jnp.float32),
            pltpu.VMEM((64 * TAPS, LANES), jnp.float32),
            pltpu.SemaphoreType.DMA((GROUP // SUB,)),
        ],
        compiler_params=grant(60),
        cost_estimate=pl.CostEstimate(flops=2000000000, bytes_accessed=4000000, transcendentals=0),
    )(start, x3, *small, *given)


def seal(ends, place, own, left, right):
    return pl.pallas_call(
        functools.partial(seal_kernel, ends),
        name="seal",
        out_shape=jax.ShapeDtypeStruct(own.shape, jnp.bfloat16),
        in_specs=[SMEM] + [VMEM] * 3,
        out_specs=VMEM,
        compiler_params=grant(4),
        cost_estimate=pl.CostEstimate(flops=1000000, bytes_accessed=300000, transcendentals=0),
    )(place, own, left, right)


def expand_kernel(where_ref, coeff_ref, out_ref):
    width = out_ref.shape[1]
    lane = lax.broadcasted_iota(jnp.int32, (FOOT, width), 1)
    dims = (((0,), (0,)), ((), ()))
    for tile in range(TILE_DEV):
        spot = where_ref[pl.ds(tile * FOOT, FOOT), :]
        hot_re = (lane == spot).astype(jnp.float32).astype(jnp.bfloat16)
        hot_im = (lane == spot + BEAMS).astype(jnp.float32).astype(jnp.bfloat16)
        c_re, c_im = coeff_ref[tile, 0], coeff_ref[tile, 1]
        dot = functools.partial(lax.dot_general, dimension_numbers=dims, preferred_element_type=jnp.float32)
        at = tile * 2 * AZ
        out_ref[pl.ds(at, AZ), :] = (dot(c_re, hot_re) - dot(c_im, hot_im)).astype(jnp.bfloat16)
        out_ref[pl.ds(at + AZ, AZ), :] = (dot(c_im, hot_re) + dot(c_re, hot_im)).astype(jnp.bfloat16)


def project_kernel(count, pieces, coeff_ref, *refs):
    sources = refs[:count]
    if sources[0].shape[0] > 64:
        sources = [ref.at[pl.ds(row, 64)] for row in range(0, sources[0].shape[0], 64) for ref in sources]
    out_hbm, tile, sems = refs[-3:]
    depth, count = 64, len(sources)
    copies = []
    for source, target, width in pieces:
        for start in range(0, width, 256):
            size = min(256, width - start)
            here = pl.ds(source + start, size)
            total = None
            for first in range(0, count, 256 // depth):
                part = sources[first : first + 256 // depth]
                data = jnp.concatenate([ref[:, here] for ref in part], axis=0)
                window = pl.ds(first * depth, len(part) * depth)
                term = jnp.dot(coeff_ref[:, window], data, preferred_element_type=jnp.float32)
                total = term if total is None else total + term
            tile[:, here] = total.astype(jnp.bfloat16)
            copy = pltpu.make_async_copy(
                tile.at[:, here], out_hbm.at[:, pl.ds(target + start, size)], sems.at[len(copies)]
            )
            copy.start()
            copies.append(copy)
    for copy in copies:
        copy.wait()


def project(coeffs, sources, image, pieces, cells):
    count = len(sources)
    width = sources[0].shape[1]
    rows, depth = coeffs.shape
    extra = [] if image is None else [image]
    return pl.pallas_call(
        functools.partial(project_kernel, count, pieces),
        out_shape=jax.ShapeDtypeStruct((rows, cells), jnp.bfloat16),
        in_specs=[VMEM] * (1 + count) + [HBM] * len(extra),
        out_specs=HBM,
        input_output_aliases={1 + count: 0} if extra else {},
        scratch_shapes=[
            pltpu.VMEM((rows, width), jnp.bfloat16),
            pltpu.SemaphoreType.DMA((sum(-(-piece[2] // 256) for piece in pieces),)),
        ],
        compiler_params=grant(10 + 2 * depth // 1024),
        cost_estimate=pl.CostEstimate(flops=2 * rows * width * depth, bytes_accessed=3000000, transcendentals=0),
    )(coeffs, *sources, *extra)


def body(echoes, shifts, tap_weights, angles, slopes, steering, footprint, tile_coeffs):
    pulses, _, cells = echoes.shape
    blocks = cells // LANES
    pulse_count = lax.axis_size("pulse")
    range_count = lax.axis_size("range")
    me = lax.axis_index("pulse")
    start_cell = lax.axis_index("range") * cells

    x4 = echoes.reshape(pulses, 2, blocks, LANES).transpose(0, 2, 1, 3)
    shared = (jnp.reshape(start_cell, (1,)), x4.reshape(pulses, 2 * blocks, LANES))
    small = (shifts, shifts[None, :], tap_weights.T, angles[None, :], slopes[None, :], steering)
    inner_a, partial = make_inner(0, *shared, small)
    inner_b, below, above, own = make_inner(1, *shared, small, partial)
    inner = [inner_a, inner_b]
    ring = [(i, (i + 1) % range_count) for i in range(range_count)]
    left = lax.ppermute(above, "range", ring)
    right = lax.ppermute(below, "range", [(target, source) for source, target in ring])
    place = jnp.reshape(lax.axis_index("range"), (1,))
    edges = seal(range_count - 1, place, own, left, right)

    entries = TILE_DEV * FOOT
    chips = pulse_count // 2
    beam_dev = pulses // SUB * BEAMS
    ids = lax.dynamic_index_in_dim(footprint.reshape(pulse_count, entries), me, 0, keepdims=False)
    owner = ids // beam_dev
    inside = ids % beam_dev
    place = 2 * ((me // 2 - owner // 2) % chips) + (me % 2 + owner % 2) % 2
    sub = inside // BEAMS
    where = place * 64 + (sub % 4) * (2 * BEAMS) + inside % BEAMS + (sub // 4) * (pulse_count * 64)
    coeffs = pl.pallas_call(
        expand_kernel,
        name="expand",
        compiler_params=grant(6),
        out_shape=jax.ShapeDtypeStruct((TILE_DEV * 2 * AZ, pulse_count * 2 * beam_dev), jnp.bfloat16),
    )(where[:, None], tile_coeffs.transpose(0, 1, 3, 2))

    swap = [(i, i ^ 1) for i in range(pulse_count)]

    def spread(own):
        sources = []
        for hop in range(chips):
            ahead = own
            if hop:
                ahead = lax.ppermute(own, "pulse", [(i, (i + 2 * hop) % pulse_count) for i in range(pulse_count)])
            sources += [ahead, lax.ppermute(ahead, "pulse", swap)]
        return sources

    spread_inner = [spread(own) for own in inner]
    spread_edges = spread(edges)
    width = cells - 2 * LANES
    image = project(coeffs, sum(spread_inner, []), None, ((0, LANES, width),), cells)
    pieces = ((0, 0, LANES), (LANES, cells - LANES, LANES))
    image = project(coeffs, spread_edges, image, pieces, cells)
    return image.reshape(TILE_DEV, 2, AZ, cells)


def solution(mesh):
    placed = (
        P(("groups", "pulse"), None, "range"),
        P(("groups", "pulse")),
        P(("groups", "pulse"), None),
        P(("groups", "pulse")),
        P(("groups", "pulse")),
        P(),
        P("groups", None),
        P(("groups", "pulse"), None, None, None),
    )
    return jax.shard_map(
        body,
        mesh=mesh,
        in_specs=placed,
        out_specs=P(("groups", "pulse"), None, None, "range"),
        check_vma=False,
    )
```

```python
import functools

import jax
import jax.numpy as jnp
from jax import lax
from jax.experimental import pallas as pl
from jax.experimental.pallas import tpu as pltpu
from jax.sharding import PartitionSpec as P

SUB = 32
BEAMS = 8
TAPS = 8
TILE_DEV = 4
FOOT = 32
AZ = 64
LANES = 128
STRIDE = 136
GRANTS = (60, 40)
GROUP = 128


def turn_by(a, b):
    return a[0] * b[0] - a[1] * b[1], a[0] * b[1] + a[1] * b[0]


def row_of(pair, index):
    return pair[0][index : index + 1], pair[1][index : index + 1]


def angle_pair(value):
    return jnp.cos(value), jnp.sin(value)


def lane_phases(slope):
    row = lax.broadcasted_iota(jnp.int32, (8, GROUP), 0)
    rows = [angle_pair(slope * row.astype(jnp.float32))]
    powers = angle_pair(slope * jnp.left_shift(8, row).astype(jnp.float32))
    for bit in range(4):
        rows = rows + [turn_by(item, row_of(powers, bit)) for item in rows]
    base = tuple(jnp.concatenate([item[part] for item in rows], axis=0).T for part in range(2))
    step = turn_by((base[0][:, 127:128], base[1][:, 127:128]), (base[0][:, 1:2], base[1][:, 1:2]))
    step = tuple(jnp.broadcast_to(part, (GROUP, LANES)) for part in step)
    return base, step


def tap_factors(start_ref, tap_ref, angle, slope, here):
    row = lax.broadcasted_iota(jnp.int32, (8, GROUP), 0)
    cell = (start_ref[0] - LANES - row).astype(jnp.float32)
    cosine, sine = angle_pair(angle + slope * cell)
    taps = tap_ref[:, here]
    return taps * cosine, taps * sine


def fill_weights(factors, steer_ref, weight_ref):
    lane = lax.broadcasted_iota(jnp.int32, (8, LANES), 1)
    steer = tuple(
        jnp.concatenate([steer_ref[part].astype(jnp.float32)] * (GROUP // SUB), axis=1) for part in range(2)
    )
    for tap in range(TAPS):
        w_re, w_im = turn_by(steer, row_of(factors, tap))
        for sub in range(GROUP // SUB):
            keep = (lane >= sub * SUB) & (lane < (sub + 1) * SUB)
            p_re = jnp.where(keep, w_re, 0.0)
            p_im = jnp.where(keep, w_im, 0.0)
            top = jnp.concatenate([p_re, 0.0 - p_im], axis=1)
            bottom = jnp.concatenate([p_im, p_re], axis=1)
            weight_ref[pl.ds(tap * 64 + sub * 16, 16), :] = jnp.concatenate([top, bottom], axis=0).astype(
                jnp.bfloat16
            )


def place_of(shift_ref, pulse, local):
    raised = shift_ref[pulse] + (LANES - 3)
    rest = raised & (LANES - 1)
    return rest, (LANES - rest) & (LANES - 1), local + 2 * STRIDE * (1 - (raised >> 7))


def split_ends(aligned, offset, last):
    lane = lax.broadcasted_iota(jnp.int32, (GROUP, LANES), 1)

    def rows(slot, part):
        return aligned[pl.ds((2 * slot + part) * STRIDE, GROUP), :]

    def first(part):
        return jnp.where(offset >= 0, rows(0, part), jnp.where(lane >= 0 - offset, rows(last + 1, part), 0.0))

    return {
        -1: lambda part: jnp.where(lane >= LANES - offset, rows(last, part), 0.0),
        0: first,
        last: lambda part: jnp.where(lane < LANES - offset, rows(last, part), 0.0),
        last + 1: lambda part: jnp.where(lane < 0 - offset, rows(last + 1, part), 0.0),
    }


def sweep(last, aligned, offset, phase, step, weight_ref, demod, products, carry, store):
    lane = lax.broadcasted_iota(jnp.int32, (8, LANES), 1)
    ends = split_ends(aligned, offset, last)
    for start in range(-1, last + 2, 2):
        for block in (start, start + 1):
            if block in ends:
                data = ends[block](0), ends[block](1)
            else:
                at = 2 * block * STRIDE
                data = aligned[pl.ds(at, GROUP), :], aligned[pl.ds(at + STRIDE, GROUP), :]
            data = turn_by(data, phase)
            phase = turn_by(phase, step)
            here = pl.ds((block + 1) * LANES, LANES)
            demod[:, here] = jnp.concatenate(data, axis=0).astype(jnp.bfloat16)
        here = pl.ds((start + 1) * LANES, 2 * LANES)
        products[:, here] = jnp.dot(weight_ref[...], demod[:, here], preferred_element_type=jnp.float32)
        for row in range(0, 64, 8):
            before = None
            if start >= 0:
                before = [carry[pl.ds(tap * 64 + row, 8), :] for tap in range(TAPS)]
            for block in (start, start + 1):
                turned = []
                for tap in range(TAPS):
                    piece = products[pl.ds(tap * 64 + row, 8), pl.ds((block + 1) * LANES, LANES)]
                    turned.append(pltpu.roll(piece, LANES - tap, 1) if tap else piece)
                if before is not None:
                    total = before[0]
                    for tap in range(1, TAPS):
                        total = total + jnp.where(lane < LANES - tap, before[tap], turned[tap])
                    store(row, block - 1, total)
                before = turned
            if start + 2 < last + 2:
                for tap in range(TAPS):
                    carry[pl.ds(tap * 64 + row, 8), :] = before[tap]
            else:
                total = before[0]
                for tap in range(1, TAPS):
                    total = total + jnp.where(lane < LANES - tap, before[tap], 0.0)
                store(row, last + 1, total)


def fetch_small(sources, targets, sems):
    copies = [pltpu.make_async_copy(s, t, sems.at[i]) for i, (s, t) in enumerate(zip(sources, targets))]
    for copy in copies:
        copy.start()
    return copies


def inner_kernel(group, start_ref, *refs):
    first_pulse = group * GROUP
    if group:
        x_ref, row_ref, tap_ref, angle_ref, slope_ref, steer_ref, shift_ref = refs[:7]
        base, small, fetches = first_pulse, [], []
        refs = refs[7:]
    else:
        given, (x_hbm, refs) = refs[1:7], (refs[0], refs[7:])
        row_ref, tap_ref, angle_ref, slope_ref, steer_ref, shift_ref, small_sems, x_ref, sems = refs[2:11]
        refs = refs[:2] + refs[11:]
        small = fetch_small(given, (row_ref, tap_ref, angle_ref, slope_ref, steer_ref, shift_ref), small_sems)
        base, fetches = 0, []
        for sub in range(GROUP // SUB):
            window = pl.ds(sub * SUB, SUB)
            fetches.append(pltpu.make_async_copy(x_hbm.at[window], x_ref.at[window], sems.at[sub]))
            fetches[-1].start()
    out_ref, partial_ref, aligned, weights, demod, products, carry = refs
    rows = x_ref.shape[1]
    for copy in small:
        copy.wait()
    here = slice(first_pulse, first_pulse + GROUP)
    slope, angle = slope_ref[:, here], angle_ref[:, here]
    phase, step = lane_phases(slope)
    fill_weights(tap_factors(start_ref, tap_ref, angle, slope, here), steer_ref, weights)
    offset = jnp.broadcast_to((row_ref[:, here] - 3).astype(jnp.float32), (GROUP, GROUP)).T.astype(jnp.int32)
    lane = lax.broadcasted_iota(jnp.int32, (rows, LANES), 1)
    for local in range(GROUP):
        if fetches and local % SUB == 0:
            fetches[local // SUB].wait()
        rest, back, first = place_of(shift_ref, first_pulse + local, local)
        data = x_ref[base + local].astype(jnp.float32)
        mixed = jnp.where(lane >= rest, data, pltpu.roll(data, rows - 2, 0))
        aligned[pl.ds(first, rows, stride=STRIDE), :] = pltpu.roll(mixed, back, 1)

    last = rows // 2 - 1
    edges = (-1, 0, last, last + 1)

    def store(row, block, total):
        if 0 < block < last:
            out_ref[pl.ds(row, 8), pl.ds((block - 1) * LANES, LANES)] = total.astype(jnp.bfloat16)
        else:
            partial_ref[pl.ds(row, 8), pl.ds(edges.index(block) * LANES, LANES)] = total

    sweep(last, aligned, offset, phase, step, weights, demod, products, carry, store)


def join_kernel(a_ref, b_ref, below_ref, above_ref):
    for row, ref in ((0, a_ref), (64, b_ref)):
        below_ref[pl.ds(row, 64), :] = ref[:, 0:LANES].astype(jnp.bfloat16)
        above_ref[pl.ds(row, 64), :] = ref[:, 3 * LANES : 4 * LANES].astype(jnp.bfloat16)


def seal_kernel(ends, place_ref, a_ref, b_ref, left_ref, right_ref, out_ref):
    for column, ref, outer in ((0, left_ref, 0), (LANES, right_ref, ends)):
        side = jnp.where(place_ref[0] == outer, 0.0, ref[...].astype(jnp.float32))
        for row, own in ((0, a_ref), (64, b_ref)):
            total = own[:, LANES + column : 2 * LANES + column] + side[row : row + 64]
            out_ref[pl.ds(row, 64), pl.ds(column, LANES)] = total.astype(jnp.bfloat16)


def grant(mebibytes):
    return pltpu.CompilerParams(vmem_limit_bytes=mebibytes * 1024 * 1024)


SMEM = pl.BlockSpec(memory_space=pltpu.SMEM)
VMEM = pl.BlockSpec(memory_space=pltpu.VMEM)
ANY = pl.BlockSpec(memory_space=pl.ANY)
HBM = pl.BlockSpec(memory_space=pltpu.HBM)


def make_inner(group, start, x3, small, shifts):
    _, rows, _ = x3.shape
    width = (rows // 2 + 2) * LANES
    fetched = []
    if not group:
        fetched = [pltpu.VMEM(item.shape, item.dtype) for item in small] + [
            pltpu.SMEM(shifts.shape, shifts.dtype),
            pltpu.SemaphoreType.DMA((len(small) + 1,)),
            pltpu.VMEM((GROUP, rows, LANES), jnp.bfloat16),
            pltpu.SemaphoreType.DMA((GROUP // SUB,)),
        ]
    specs = [VMEM] * (1 + len(small)) + [SMEM] if group else [HBM] * (2 + len(small))
    return pl.pallas_call(
        functools.partial(inner_kernel, group),
        out_shape=(
            jax.ShapeDtypeStruct((64, width - 4 * LANES), jnp.bfloat16),
            jax.ShapeDtypeStruct((64, 4 * LANES), jnp.float32),
        ),
        in_specs=[SMEM] + specs,
        out_specs=(VMEM, VMEM),
        scratch_shapes=fetched
        + [
            pltpu.VMEM(((rows + 2) * STRIDE, LANES), jnp.float32),
            pltpu.VMEM((64 * TAPS, 2 * GROUP), jnp.bfloat16),
            pltpu.VMEM((2 * GROUP, width), jnp.bfloat16),
            pltpu.VMEM((64 * TAPS, width), jnp.float32),
            pltpu.VMEM((64 * TAPS, LANES), jnp.float32),
        ],
        compiler_params=grant(GRANTS[group]),
        cost_estimate=pl.CostEstimate(flops=2000000000, bytes_accessed=4000000, transcendentals=0),
    )(start, x3, *small, shifts)


def join(part_a, part_b):
    side = jax.ShapeDtypeStruct((128, LANES), jnp.bfloat16)
    return pl.pallas_call(
        join_kernel,
        name="join",
        out_shape=(side, side),
        in_specs=[VMEM, VMEM],
        out_specs=(VMEM, VMEM),
        compiler_params=grant(4),
        cost_estimate=pl.CostEstimate(flops=1000000, bytes_accessed=300000, transcendentals=0),
    )(part_a, part_b)


def seal(ends, place, part_a, part_b, left, right):
    return pl.pallas_call(
        functools.partial(seal_kernel, ends),
        name="seal",
        out_shape=jax.ShapeDtypeStruct((128, 2 * LANES), jnp.bfloat16),
        in_specs=[SMEM] + [VMEM] * 4,
        out_specs=VMEM,
        compiler_params=grant(4),
        cost_estimate=pl.CostEstimate(flops=1000000, bytes_accessed=300000, transcendentals=0),
    )(place, part_a, part_b, left, right)


def expand_kernel(where_ref, coeff_ref, out_ref):
    width = out_ref.shape[1]
    lane = lax.broadcasted_iota(jnp.int32, (FOOT, width), 1)
    dims = (((0,), (0,)), ((), ()))
    for tile in range(TILE_DEV):
        spot = where_ref[pl.ds(tile * FOOT, FOOT), :]
        hot_re = (lane == spot).astype(jnp.float32).astype(jnp.bfloat16)
        hot_im = (lane == spot + BEAMS).astype(jnp.float32).astype(jnp.bfloat16)
        c_re, c_im = coeff_ref[tile, 0], coeff_ref[tile, 1]
        dot = functools.partial(lax.dot_general, dimension_numbers=dims, preferred_element_type=jnp.float32)
        at = tile * 2 * AZ
        out_ref[pl.ds(at, AZ), :] = (dot(c_re, hot_re) - dot(c_im, hot_im)).astype(jnp.bfloat16)
        out_ref[pl.ds(at + AZ, AZ), :] = (dot(c_im, hot_re) + dot(c_re, hot_im)).astype(jnp.bfloat16)


def project_kernel(members, coeff_ref, *refs):
    inner, edges = refs[: 2 * members], refs[2 * members : 3 * members]
    out_hbm, tile, sems = refs[3 * members :]
    cells = tile.shape[1]
    width = cells - 2 * LANES
    edges = [ref.at[pl.ds(row, 64)] for row in (0, 64) for ref in edges]
    jobs = [(inner, start, LANES + start, ((LANES + start, 256, 0),)) for start in range(0, width, 256)]
    jobs.append((edges, 0, 0, ((0, LANES, 0), (cells - LANES, LANES, LANES))))
    copies = []
    for sources, start, _, targets in jobs:
        here = pl.ds(start, 256)
        total = None
        for first in range(0, 2 * members, 4):
            data = jnp.concatenate([ref[:, here] for ref in sources[first : first + 4]], axis=0)
            term = jnp.dot(coeff_ref[:, pl.ds(first * 64, 256)], data, preferred_element_type=jnp.float32)
            total = term if total is None else total + term
        total = total.astype(jnp.bfloat16)
        for target, size, skip in targets:
            there = pl.ds(target, size)
            tile[:, there] = total[:, skip : skip + size]
            copies.append(pltpu.make_async_copy(tile.at[:, there], out_hbm.at[:, there], sems.at[len(copies)]))
            copies[-1].start()
    for copy in copies:
        copy.wait()


def project(coeffs, inner, edges, cells):
    rows, depth = coeffs.shape
    return pl.pallas_call(
        functools.partial(project_kernel, len(edges)),
        name="project",
        out_shape=jax.ShapeDtypeStruct((rows, cells), jnp.bfloat16),
        in_specs=[VMEM] * (1 + len(inner) + len(edges)),
        out_specs=HBM,
        scratch_shapes=[
            pltpu.VMEM((rows, cells), jnp.bfloat16),
            pltpu.SemaphoreType.DMA(((cells - 2 * LANES) // 256 + 2,)),
        ],
        compiler_params=grant(10 + 8 * depth // 1024),
        cost_estimate=pl.CostEstimate(flops=2 * rows * cells * depth, bytes_accessed=3000000, transcendentals=0),
    )(coeffs, *inner, *edges)


def body(echoes, shifts, tap_weights, angles, slopes, steering, footprint, tile_coeffs):
    pulses, _, cells = echoes.shape
    blocks = cells // LANES
    pulse_count = lax.axis_size("pulse")
    range_count = lax.axis_size("range")
    me = lax.axis_index("pulse")
    start_cell = lax.axis_index("range") * cells

    x4 = echoes.reshape(pulses, 2, blocks, LANES).transpose(0, 2, 1, 3)
    shared = (jnp.reshape(start_cell, (1,)), x4.reshape(pulses, 2 * blocks, LANES))
    small = (shifts[None, :], tap_weights.T, angles[None, :], slopes[None, :], steering)
    inner_a, part_a = make_inner(0, *shared, small, shifts)
    inner_b, part_b = make_inner(1, *shared, small, shifts)
    inner = [inner_a, inner_b]
    below, above = join(part_a, part_b)
    ring = [(i, (i + 1) % range_count) for i in range(range_count)]
    left = lax.ppermute(above, "range", ring)
    right = lax.ppermute(below, "range", [(target, source) for source, target in ring])
    place = jnp.reshape(lax.axis_index("range"), (1,))
    edges = seal(range_count - 1, place, part_a, part_b, left, right)

    entries = TILE_DEV * FOOT
    chips = pulse_count // 2
    beam_dev = pulses // SUB * BEAMS
    ids = lax.dynamic_index_in_dim(footprint.reshape(pulse_count, entries), me, 0, keepdims=False)
    owner = ids // beam_dev
    inside = ids % beam_dev
    place = 2 * ((me // 2 - owner // 2) % chips) + (me % 2 + owner % 2) % 2
    sub = inside // BEAMS
    where = place * 64 + (sub % 4) * (2 * BEAMS) + inside % BEAMS + (sub // 4) * (pulse_count * 64)
    coeffs = pl.pallas_call(
        expand_kernel,
        name="expand",
        compiler_params=grant(6),
        out_shape=jax.ShapeDtypeStruct((TILE_DEV * 2 * AZ, pulse_count * 2 * beam_dev), jnp.bfloat16),
    )(where[:, None], tile_coeffs.transpose(0, 1, 3, 2))

    swap = [(i, i ^ 1) for i in range(pulse_count)]

    def spread(own):
        sources = []
        for hop in range(chips):
            ahead = own
            if hop:
                ahead = lax.ppermute(own, "pulse", [(i, (i + 2 * hop) % pulse_count) for i in range(pulse_count)])
            sources += [ahead, lax.ppermute(ahead, "pulse", swap)]
        return sources

    spread_inner = [spread(own) for own in inner]
    spread_edges = spread(edges)
    image = project(coeffs, sum(spread_inner, []), spread_edges, cells)
    return image.reshape(TILE_DEV, 2, AZ, cells)


def solution(mesh):
    placed = (
        P(("groups", "pulse"), None, "range"),
        P(("groups", "pulse")),
        P(("groups", "pulse"), None),
        P(("groups", "pulse")),
        P(("groups", "pulse")),
        P(),
        P("groups", None),
        P(("groups", "pulse"), None, None, None),
    )
    return jax.shard_map(
        body,
        mesh=mesh,
        in_specs=placed,
        out_specs=P(("groups", "pulse"), None, None, "range"),
        check_vma=False,
    )
```

```python
import functools

import jax
import jax.numpy as jnp
from jax import lax
from jax.experimental import pallas as pl
from jax.experimental.pallas import tpu as pltpu
from jax.sharding import PartitionSpec as P

SUB = 32
BEAMS = 8
TAPS = 8
TILE_DEV = 4
FOOT = 32
AZ = 64
LANES = 128
STRIDE = 136
GRANTS = (60, 40)
GROUP = 128


def turn_by(a, b):
    return a[0] * b[0] - a[1] * b[1], a[0] * b[1] + a[1] * b[0]


def row_of(pair, index):
    return pair[0][index : index + 1], pair[1][index : index + 1]


def angle_pair(value):
    return jnp.cos(value), jnp.sin(value)


def lane_phases(slope):
    row = lax.broadcasted_iota(jnp.int32, (8, GROUP), 0)
    rows = [angle_pair(slope * row.astype(jnp.float32))]
    powers = angle_pair(slope * jnp.left_shift(8, row).astype(jnp.float32))
    for bit in range(4):
        rows = rows + [turn_by(item, row_of(powers, bit)) for item in rows]
    base = tuple(jnp.concatenate([item[part] for item in rows], axis=0).T for part in range(2))
    step = turn_by((base[0][:, 127:128], base[1][:, 127:128]), (base[0][:, 1:2], base[1][:, 1:2]))
    step = tuple(jnp.broadcast_to(part, (GROUP, LANES)) for part in step)
    return base, step


def tap_factors(start_ref, tap_ref, angle, slope, here):
    row = lax.broadcasted_iota(jnp.int32, (8, GROUP), 0)
    cell = (start_ref[0] - LANES - row).astype(jnp.float32)
    cosine, sine = angle_pair(angle + slope * cell)
    taps = tap_ref[:, here]
    return taps * cosine, taps * sine


def fill_weights(factors, steer_ref, weight_ref, per_row):
    lane = lax.broadcasted_iota(jnp.int32, (8, LANES), 1)
    steer = tuple(
        jnp.concatenate([steer_ref[part].astype(jnp.float32)] * (GROUP // SUB), axis=1) for part in range(2)
    )
    for tap in range(TAPS):
        w_re, w_im = turn_by(steer, row_of(factors, tap))
        for sub in range(GROUP // SUB):
            keep = (lane >= sub * SUB) & (lane < (sub + 1) * SUB)
            p_re = jnp.where(keep, w_re, 0.0)
            p_im = jnp.where(keep, w_im, 0.0)
            top = jnp.concatenate([p_re, 0.0 - p_im], axis=1)
            bottom = jnp.concatenate([p_im, p_re], axis=1)
            column = tap % per_row * 2 * GROUP
            spot = pl.ds(tap // per_row * 64 + sub * 16, 16), pl.ds(column, 2 * GROUP)
            weight_ref[spot] = jnp.concatenate([top, bottom], axis=0).astype(jnp.bfloat16)


def place_of(shift_ref, pulse, local):
    raised = shift_ref[pulse] + (LANES - 3)
    rest = raised & (LANES - 1)
    return rest, (LANES - rest) & (LANES - 1), local + 2 * STRIDE * (1 - (raised >> 7))


def split_ends(aligned, offset, last):
    lane = lax.broadcasted_iota(jnp.int32, (GROUP, LANES), 1)

    def rows(slot, part):
        return aligned[pl.ds((2 * slot + part) * STRIDE, GROUP), :]

    def first(part):
        return jnp.where(offset >= 0, rows(0, part), jnp.where(lane >= 0 - offset, rows(last + 1, part), 0.0))

    return {
        -1: lambda part: jnp.where(lane >= LANES - offset, rows(last, part), 0.0),
        0: first,
        last: lambda part: jnp.where(lane < LANES - offset, rows(last, part), 0.0),
        last + 1: lambda part: jnp.where(lane < 0 - offset, rows(last + 1, part), 0.0),
    }


def sweep(last, aligned, offset, phase, step, weight_ref, demod, products, carry, store):
    lane = lax.broadcasted_iota(jnp.int32, (8, LANES), 1)
    ends = split_ends(aligned, offset, last)
    for start in range(-1, last + 2, 2):
        for block in (start, start + 1):
            if block in ends:
                data = ends[block](0), ends[block](1)
            else:
                at = 2 * block * STRIDE
                data = aligned[pl.ds(at, GROUP), :], aligned[pl.ds(at + STRIDE, GROUP), :]
            data = turn_by(data, phase)
            phase = turn_by(phase, step)
            here = pl.ds((block + 1) * LANES, LANES)
            demod[:, here] = jnp.concatenate(data, axis=0).astype(jnp.bfloat16)
        here = pl.ds((start + 1) * LANES, 2 * LANES)
        products[:, here] = jnp.dot(weight_ref[...], demod[:, here], preferred_element_type=jnp.float32)
        for row in range(0, 64, 8):
            before = None
            if start >= 0:
                before = [carry[pl.ds(tap * 64 + row, 8), :] for tap in range(TAPS)]
            for block in (start, start + 1):
                turned = []
                for tap in range(TAPS):
                    piece = products[pl.ds(tap * 64 + row, 8), pl.ds((block + 1) * LANES, LANES)]
                    turned.append(pltpu.roll(piece, LANES - tap, 1) if tap else piece)
                if before is not None:
                    total = before[0]
                    for tap in range(1, TAPS):
                        total = total + jnp.where(lane < LANES - tap, before[tap], turned[tap])
                    store(row, block - 1, total)
                before = turned
            if start + 2 < last + 2:
                for tap in range(TAPS):
                    carry[pl.ds(tap * 64 + row, 8), :] = before[tap]
            else:
                total = before[0]
                for tap in range(1, TAPS):
                    total = total + jnp.where(lane < LANES - tap, before[tap], 0.0)
                store(row, last + 1, total)


def sweep_pairs(last, aligned, offset, phase, step, weight_ref, demod, products, carry, store):
    lane = lax.broadcasted_iota(jnp.int32, (8, LANES), 1)
    wide = lax.broadcasted_iota(jnp.int32, (2 * GROUP, LANES), 1)
    ends = split_ends(aligned, offset, last)
    pairs = TAPS // 2

    def mixed(before, turned):
        total = before[0]
        for pair in range(1, pairs):
            later = turned[pair] if turned else 0.0
            total = total + jnp.where(lane < LANES - 2 * pair, before[pair], later)
        return total

    held = None
    for block in range(-1, last + 3):
        if block > last + 1:
            data = jnp.zeros((2 * GROUP, LANES), jnp.float32)
        else:
            if block in ends:
                data = ends[block](0), ends[block](1)
            else:
                at = 2 * block * STRIDE
                data = aligned[pl.ds(at, GROUP), :], aligned[pl.ds(at + STRIDE, GROUP), :]
            data = jnp.concatenate(turn_by(data, phase), axis=0)
            phase = turn_by(phase, step)
            demod[0 : 2 * GROUP, pl.ds((block + 1) * LANES, LANES)] = data.astype(jnp.bfloat16)
        if held is not None:
            further = pltpu.roll(jnp.where(wide >= 1, held, data).astype(jnp.bfloat16), LANES - 1, 1)
            demod[2 * GROUP : 4 * GROUP, pl.ds(block * LANES, LANES)] = further
        held = data
        start = block - 2
        if start < -1 or start % 2 == 0:
            continue
        here = pl.ds((start + 1) * LANES, 2 * LANES)
        products[:, here] = jnp.dot(weight_ref[...], demod[:, here], preferred_element_type=jnp.float32)
        for row in range(0, 64, 8):
            before = None
            if start >= 0:
                before = [carry[pl.ds(pair * 64 + row, 8), :] for pair in range(pairs)]
            for tile in (start, start + 1):
                turned = []
                for pair in range(pairs):
                    piece = products[pl.ds(pair * 64 + row, 8), pl.ds((tile + 1) * LANES, LANES)]
                    turned.append(pltpu.roll(piece, LANES - 2 * pair, 1) if pair else piece)
                if before is not None:
                    store(row, tile - 1, mixed(before, turned))
                before = turned
            if start + 2 < last + 2:
                for pair in range(pairs):
                    carry[pl.ds(pair * 64 + row, 8), :] = before[pair]
            else:
                store(row, last + 1, mixed(before, None))


def fetch_small(sources, targets, sems):
    copies = [pltpu.make_async_copy(s, t, sems.at[i]) for i, (s, t) in enumerate(zip(sources, targets))]
    for copy in copies:
        copy.start()
    return copies


def inner_kernel(group, start_ref, *refs):
    first_pulse = group * GROUP
    if group:
        x_ref, row_ref, tap_ref, angle_ref, slope_ref, steer_ref, shift_ref = refs[:7]
        base, small, fetches = first_pulse, [], []
        refs = refs[7:]
    else:
        given, (x_hbm, refs) = refs[1:7], (refs[0], refs[7:])
        row_ref, tap_ref, angle_ref, slope_ref, steer_ref, shift_ref, small_sems, x_ref, sems = refs[2:11]
        refs = refs[:2] + refs[11:]
        small = fetch_small(given, (row_ref, tap_ref, angle_ref, slope_ref, steer_ref, shift_ref), small_sems)
        base, fetches = 0, []
        for sub in range(GROUP // SUB):
            window = pl.ds(sub * SUB, SUB)
            fetches.append(pltpu.make_async_copy(x_hbm.at[window], x_ref.at[window], sems.at[sub]))
            fetches[-1].start()
    out_ref, partial_ref, aligned, weights, demod, products, carry = refs
    rows = x_ref.shape[1]
    for copy in small:
        copy.wait()
    here = slice(first_pulse, first_pulse + GROUP)
    slope, angle = slope_ref[:, here], angle_ref[:, here]
    phase, step = lane_phases(slope)
    fill_weights(tap_factors(start_ref, tap_ref, angle, slope, here), steer_ref, weights, 1 if group else 2)
    offset = jnp.broadcast_to((row_ref[:, here] - 3).astype(jnp.float32), (GROUP, GROUP)).T.astype(jnp.int32)
    lane = lax.broadcasted_iota(jnp.int32, (rows, LANES), 1)
    for local in range(GROUP):
        if fetches and local % SUB == 0:
            fetches[local // SUB].wait()
        rest, back, first = place_of(shift_ref, first_pulse + local, local)
        data = x_ref[base + local].astype(jnp.float32)
        mixed = jnp.where(lane >= rest, data, pltpu.roll(data, rows - 2, 0))
        aligned[pl.ds(first, rows, stride=STRIDE), :] = pltpu.roll(mixed, back, 1)

    last = rows // 2 - 1
    edges = (-1, 0, last, last + 1)

    def store(row, block, total):
        if 0 < block < last:
            out_ref[pl.ds(row, 8), pl.ds((block - 1) * LANES, LANES)] = total.astype(jnp.bfloat16)
        else:
            partial_ref[pl.ds(row, 8), pl.ds(edges.index(block) * LANES, LANES)] = total

    run = sweep if group else sweep_pairs
    run(last, aligned, offset, phase, step, weights, demod, products, carry, store)


def join_kernel(a_ref, b_ref, below_ref, above_ref):
    for row, ref in ((0, a_ref), (64, b_ref)):
        below_ref[pl.ds(row, 64), :] = ref[:, 0:LANES].astype(jnp.bfloat16)
        above_ref[pl.ds(row, 64), :] = ref[:, 3 * LANES : 4 * LANES].astype(jnp.bfloat16)


def seal_kernel(ends, place_ref, a_ref, b_ref, left_ref, right_ref, out_ref):
    for column, ref, outer in ((0, left_ref, 0), (LANES, right_ref, ends)):
        side = jnp.where(place_ref[0] == outer, 0.0, ref[...].astype(jnp.float32))
        for row, own in ((0, a_ref), (64, b_ref)):
            total = own[:, LANES + column : 2 * LANES + column] + side[row : row + 64]
            out_ref[pl.ds(row, 64), pl.ds(column, LANES)] = total.astype(jnp.bfloat16)


def grant(mebibytes):
    return pltpu.CompilerParams(vmem_limit_bytes=mebibytes * 1024 * 1024)


SMEM = pl.BlockSpec(memory_space=pltpu.SMEM)
VMEM = pl.BlockSpec(memory_space=pltpu.VMEM)
ANY = pl.BlockSpec(memory_space=pl.ANY)
HBM = pl.BlockSpec(memory_space=pltpu.HBM)


def make_inner(group, start, x3, small, shifts):
    _, rows, _ = x3.shape
    width = (rows // 2 + 2) * LANES
    per_row = 1 if group else 2
    fetched = []
    if not group:
        fetched = [pltpu.VMEM(item.shape, item.dtype) for item in small] + [
            pltpu.SMEM(shifts.shape, shifts.dtype),
            pltpu.SemaphoreType.DMA((len(small) + 1,)),
            pltpu.VMEM((GROUP, rows, LANES), jnp.bfloat16),
            pltpu.SemaphoreType.DMA((GROUP // SUB,)),
        ]
    specs = [VMEM] * (1 + len(small)) + [SMEM] if group else [HBM] * (2 + len(small))
    return pl.pallas_call(
        functools.partial(inner_kernel, group),
        out_shape=(
            jax.ShapeDtypeStruct((64, width - 4 * LANES), jnp.bfloat16),
            jax.ShapeDtypeStruct((64, 4 * LANES), jnp.float32),
        ),
        in_specs=[SMEM] + specs,
        out_specs=(VMEM, VMEM),
        scratch_shapes=fetched
        + [
            pltpu.VMEM(((rows + 2) * STRIDE, LANES), jnp.float32),
            pltpu.VMEM((64 * TAPS // per_row, 2 * GROUP * per_row), jnp.bfloat16),
            pltpu.VMEM((2 * GROUP * per_row, width), jnp.bfloat16),
            pltpu.VMEM((64 * TAPS // per_row, width), jnp.float32),
            pltpu.VMEM((64 * TAPS // per_row, LANES), jnp.float32),
        ],
        compiler_params=grant(GRANTS[group]),
        cost_estimate=pl.CostEstimate(flops=2000000000, bytes_accessed=4000000, transcendentals=0),
    )(start, x3, *small, shifts)


def join(part_a, part_b):
    side = jax.ShapeDtypeStruct((128, LANES), jnp.bfloat16)
    return pl.pallas_call(
        join_kernel,
        name="join",
        out_shape=(side, side),
        in_specs=[VMEM, VMEM],
        out_specs=(VMEM, VMEM),
        compiler_params=grant(4),
        cost_estimate=pl.CostEstimate(flops=1000000, bytes_accessed=300000, transcendentals=0),
    )(part_a, part_b)


def seal(ends, place, part_a, part_b, left, right):
    return pl.pallas_call(
        functools.partial(seal_kernel, ends),
        name="seal",
        out_shape=jax.ShapeDtypeStruct((128, 2 * LANES), jnp.bfloat16),
        in_specs=[SMEM] + [VMEM] * 4,
        out_specs=VMEM,
        compiler_params=grant(4),
        cost_estimate=pl.CostEstimate(flops=1000000, bytes_accessed=300000, transcendentals=0),
    )(place, part_a, part_b, left, right)


def expand_kernel(where_ref, coeff_ref, out_ref):
    width = out_ref.shape[1]
    lane = lax.broadcasted_iota(jnp.int32, (FOOT, width), 1)
    dims = (((0,), (0,)), ((), ()))
    for tile in range(TILE_DEV):
        spot = where_ref[pl.ds(tile * FOOT, FOOT), :]
        hot_re = (lane == spot).astype(jnp.float32).astype(jnp.bfloat16)
        hot_im = (lane == spot + BEAMS).astype(jnp.float32).astype(jnp.bfloat16)
        c_re, c_im = coeff_ref[tile, 0], coeff_ref[tile, 1]
        dot = functools.partial(lax.dot_general, dimension_numbers=dims, preferred_element_type=jnp.float32)
        at = tile * 2 * AZ
        out_ref[pl.ds(at, AZ), :] = (dot(c_re, hot_re) - dot(c_im, hot_im)).astype(jnp.bfloat16)
        out_ref[pl.ds(at + AZ, AZ), :] = (dot(c_im, hot_re) + dot(c_re, hot_im)).astype(jnp.bfloat16)


def project_kernel(members, coeff_ref, *refs):
    inner, edges = refs[: 2 * members], refs[2 * members : 3 * members]
    out_hbm, tile, sems = refs[3 * members :]
    cells = tile.shape[1]
    width = cells - 2 * LANES
    edges = [ref.at[pl.ds(row, 64)] for row in (0, 64) for ref in edges]
    jobs = [(inner, start, LANES + start, ((LANES + start, 256, 0),)) for start in range(0, width, 256)]
    jobs.append((edges, 0, 0, ((0, LANES, 0), (cells - LANES, LANES, LANES))))
    copies = []
    for sources, start, _, targets in jobs:
        here = pl.ds(start, 256)
        total = None
        for first in range(0, 2 * members, 4):
            data = jnp.concatenate([ref[:, here] for ref in sources[first : first + 4]], axis=0)
            term = jnp.dot(coeff_ref[:, pl.ds(first * 64, 256)], data, preferred_element_type=jnp.float32)
            total = term if total is None else total + term
        total = total.astype(jnp.bfloat16)
        for target, size, skip in targets:
            there = pl.ds(target, size)
            tile[:, there] = total[:, skip : skip + size]
            copies.append(pltpu.make_async_copy(tile.at[:, there], out_hbm.at[:, there], sems.at[len(copies)]))
            copies[-1].start()
    for copy in copies:
        copy.wait()


def project(coeffs, inner, edges, cells):
    rows, depth = coeffs.shape
    return pl.pallas_call(
        functools.partial(project_kernel, len(edges)),
        name="project",
        out_shape=jax.ShapeDtypeStruct((rows, cells), jnp.bfloat16),
        in_specs=[VMEM] * (1 + len(inner) + len(edges)),
        out_specs=HBM,
        scratch_shapes=[
            pltpu.VMEM((rows, cells), jnp.bfloat16),
            pltpu.SemaphoreType.DMA(((cells - 2 * LANES) // 256 + 2,)),
        ],
        compiler_params=grant(10 + 8 * depth // 1024),
        cost_estimate=pl.CostEstimate(flops=2 * rows * cells * depth, bytes_accessed=3000000, transcendentals=0),
    )(coeffs, *inner, *edges)


def body(echoes, shifts, tap_weights, angles, slopes, steering, footprint, tile_coeffs):
    pulses, _, cells = echoes.shape
    blocks = cells // LANES
    pulse_count = lax.axis_size("pulse")
    range_count = lax.axis_size("range")
    me = lax.axis_index("pulse")
    start_cell = lax.axis_index("range") * cells

    x4 = echoes.reshape(pulses, 2, blocks, LANES).transpose(0, 2, 1, 3)
    shared = (jnp.reshape(start_cell, (1,)), x4.reshape(pulses, 2 * blocks, LANES))
    small = (shifts[None, :], tap_weights.T, angles[None, :], slopes[None, :], steering)
    inner_a, part_a = make_inner(0, *shared, small, shifts)
    inner_b, part_b = make_inner(1, *shared, small, shifts)
    inner = [inner_a, inner_b]
    below, above = join(part_a, part_b)
    ring = [(i, (i + 1) % range_count) for i in range(range_count)]
    left = lax.ppermute(above, "range", ring)
    right = lax.ppermute(below, "range", [(target, source) for source, target in ring])
    place = jnp.reshape(lax.axis_index("range"), (1,))
    edges = seal(range_count - 1, place, part_a, part_b, left, right)

    entries = TILE_DEV * FOOT
    chips = pulse_count // 2
    beam_dev = pulses // SUB * BEAMS
    ids = lax.dynamic_index_in_dim(footprint.reshape(pulse_count, entries), me, 0, keepdims=False)
    owner = ids // beam_dev
    inside = ids % beam_dev
    place = 2 * ((me // 2 - owner // 2) % chips) + (me % 2 + owner % 2) % 2
    sub = inside // BEAMS
    where = place * 64 + (sub % 4) * (2 * BEAMS) + inside % BEAMS + (sub // 4) * (pulse_count * 64)
    coeffs = pl.pallas_call(
        expand_kernel,
        name="expand",
        compiler_params=grant(6),
        out_shape=jax.ShapeDtypeStruct((TILE_DEV * 2 * AZ, pulse_count * 2 * beam_dev), jnp.bfloat16),
    )(where[:, None], tile_coeffs.transpose(0, 1, 3, 2))

    swap = [(i, i ^ 1) for i in range(pulse_count)]

    def spread(own):
        sources = []
        for hop in range(chips):
            ahead = own
            if hop:
                ahead = lax.ppermute(own, "pulse", [(i, (i + 2 * hop) % pulse_count) for i in range(pulse_count)])
            sources += [ahead, lax.ppermute(ahead, "pulse", swap)]
        return sources

    spread_inner = [spread(own) for own in inner]
    spread_edges = spread(edges)
    image = project(coeffs, sum(spread_inner, []), spread_edges, cells)
    return image.reshape(TILE_DEV, 2, AZ, cells)


def solution(mesh):
    placed = (
        P(("groups", "pulse"), None, "range"),
        P(("groups", "pulse")),
        P(("groups", "pulse"), None),
        P(("groups", "pulse")),
        P(("groups", "pulse")),
        P(),
        P("groups", None),
        P(("groups", "pulse"), None, None, None),
    )
    return jax.shard_map(
        body,
        mesh=mesh,
        in_specs=placed,
        out_specs=P(("groups", "pulse"), None, None, "range"),
        check_vma=False,
    )
```
